32 devices in a mesh: ctx: 8 (over z, y), head: 4 (over x, core).
Axes of the slice: x: 2, y: 2, z: 4, core: 2. Of those that a mesh axis runs over, the one named last changes fastest.
Arguments:
- qkv: bfloat16 [3, 4096, 5120], P(None, 'ctx', 'head'), may hold values from -8 to 8
- step_size: float32 [4096, 8], P('ctx', 'head'), may hold values from 0.01 to 0.1
- fast_in: bfloat16 [8, 640, 1024], P('head'), may hold values from -1 to 1
- fast_out: bfloat16 [8, 512, 640], P('head'), may hold values from -1 to 1
Outputs:
- mixed: bfloat16 [4096, 5120], P('ctx', 'head')
The draws below stay inside these ranges and needn't reach their ends.
All inputs are finite; a program needn't handle non-finite values.
Results may differ from the reference program's by a relative error of at most 0.0087.
Values may be sent and summed in bfloat16 or wider, within the bound.
No kernel may reach another device: no remote copies, remote signals or barrier semaphores. Data moves between devices by JAX's collectives and lax.ppermute only.
A program may use at most 128 MiB of HBM per device.

```python
import math
import jax
import jax.numpy as jnp
from jax import lax

D = 5120
ADIM = 128
FW_HEADS = 8
FH = 512
HD = 640
TOK_DEV = 512
TOKENS = 4096
WINDOW = 1024


def base_values(key_base, full_shape):
    return jnp.clip(jax.random.normal(key_base, full_shape, jnp.float32), -2.5, 2.5)


def column_scaled(key, full_shape, fan_in):
    key_base, key_scale = jax.random.split(key)
    base_draw = base_values(key_base, full_shape)
    scales = jnp.exp(jax.random.uniform(key_scale, (full_shape[0], 1, full_shape[2]), jnp.float32, math.log(0.3), math.log(3.0)))
    return base_draw * scales * fan_in ** (-0.5)


def draw_fast_in(key, part):
    key_base, key_scale, key_jitter = jax.random.split(jax.random.fold_in(key, 11), 3)
    full_shape = (FW_HEADS, HD, 2 * FH)
    base_draw = base_values(key_base, full_shape)
    gate_scale = jnp.exp(jax.random.uniform(key_scale, (FW_HEADS, 1, FH), jnp.float32, math.log(0.3), math.log(3.0)))
    jitter = jnp.exp(jax.random.uniform(key_jitter, (FW_HEADS, 1, FH), jnp.float32, math.log(0.6), math.log(0.9)))
    up_scale = jitter / gate_scale
    scales = jnp.concatenate([gate_scale, up_scale], axis=2)
    return (base_draw * scales * HD ** (-0.5)).astype(jnp.bfloat16)


def draw_fast_out(key, part):
    return column_scaled(jax.random.fold_in(key, 13), (FW_HEADS, FH, HD), FH).astype(jnp.bfloat16)


def draw_qkv(key, part):
    key_base = jax.random.fold_in(jax.random.fold_in(key, 7), 0)
    full_shape = (3, TOKENS, D)
    base_draw = jnp.clip(1.5 * jax.random.normal(key_base, full_shape, jnp.float32), -8.0, 8.0)
    return base_draw.astype(jnp.bfloat16)


def block_levels(stream_key, extent, pieces, least, largest):
    level = 1.0
    for axis_at, parts in pieces:
        draws = jax.random.uniform(jax.random.fold_in(jax.random.fold_in(stream_key, 6), axis_at), (parts,), jnp.float32, least / len(pieces), largest / len(pieces))
        level = level * jnp.repeat(jnp.exp(draws), extent[axis_at] // parts).reshape((-1,) + (1,) * (len(extent) - 1 - axis_at))
    return level


def setup_inputs(seed: int = 0) -> dict:
    streams_of = jax.random.split(jax.random.key(seed), 5)
    return {
        "qkv": draw_qkv(jax.random.fold_in(streams_of[4], 71), 0),
        "step_size": jnp.clip(jnp.exp(math.log(0.1) - 2.3025851 * jax.random.uniform(streams_of[1], (TOKENS, FW_HEADS), jnp.float32) ** block_levels(streams_of[1], (TOKENS, FW_HEADS), ((0, 8), (1, 4)), -0.2, 0.2)), 0.01, 0.1),
        "fast_in": draw_fast_in(jax.random.fold_in(streams_of[4], 71), 0),
        "fast_out": draw_fast_out(jax.random.fold_in(streams_of[4], 71), 0),
    }


EPS = 1e-06

def silu_parts(gate_part):
    sigmoid_part = jax.nn.sigmoid(gate_part)
    return (gate_part * sigmoid_part, sigmoid_part * (1.0 + gate_part * (1.0 - sigmoid_part)))

def renorm(weight, update, norm_axis):
    old_value = weight.astype(jnp.float32)
    moved_value = old_value + update
    old_norm = jnp.sqrt(lax.optimization_barrier(jnp.sum(old_value * old_value, axis=norm_axis, keepdims=True)))
    new_norm = jnp.sqrt(lax.optimization_barrier(jnp.sum(moved_value * moved_value, axis=norm_axis, keepdims=True)))
    return (moved_value * (old_norm / (new_norm + EPS))).astype(jnp.bfloat16)

def fast_head(inputs):
    queries, key_rows, values, rates, w_in, w_out = inputs
    projected = jnp.dot(key_rows, w_in, preferred_element_type=jnp.float32)
    gate_part = projected[:, :FH]
    up_part = projected[:, FH:]
    activated, slope_part = silu_parts(gate_part)
    hidden = (activated * up_part).astype(jnp.bfloat16)
    scaled = (rates[:, None] * values.astype(jnp.float32)).astype(jnp.bfloat16)
    back_part = jnp.dot(scaled, w_out.T, preferred_element_type=jnp.float32)
    pre_grad = jnp.concatenate([back_part * up_part * slope_part, back_part * activated], axis=1).astype(jnp.bfloat16)
    grad_in = jnp.dot(key_rows.T, pre_grad, preferred_element_type=jnp.float32)
    grad_out = jnp.dot(hidden.T, scaled, preferred_element_type=jnp.float32)
    factor = TOKENS ** (-0.5)
    new_in = renorm(w_in, grad_in * factor, 0)
    new_out = renorm(w_out, grad_out * factor, 0)
    query_proj = jnp.dot(queries, new_in, preferred_element_type=jnp.float32)
    query_act, unused_slope = silu_parts(query_proj[:, :FH])
    query_hidden = (query_act * query_proj[:, FH:]).astype(jnp.bfloat16)
    return jnp.dot(query_hidden, new_out, preferred_element_type=jnp.float32)

def band_attention(queries, key_rows, values):
    head_count = D // ADIM
    block_rows = TOK_DEV
    block_count = TOKENS // TOK_DEV
    padding = jnp.zeros((WINDOW, D), jnp.bfloat16)
    key_padded = jnp.concatenate([padding, key_rows], axis=0)
    value_padded = jnp.concatenate([padding, values], axis=0)
    row_pos = lax.broadcasted_iota(jnp.int32, (block_rows, block_rows + WINDOW), 0)
    col_pos = lax.broadcasted_iota(jnp.int32, (block_rows, block_rows + WINDOW), 1)

    def one_block(block_index):
        row_start = (block_index * block_rows).astype(jnp.int32)
        query_block = lax.dynamic_slice_in_dim(queries, row_start, block_rows, 0).reshape(block_rows, head_count, ADIM).astype(jnp.float32)
        key_block = lax.dynamic_slice_in_dim(key_padded, row_start, block_rows + WINDOW, 0).reshape(block_rows + WINDOW, head_count, ADIM).astype(jnp.float32)
        value_block = lax.dynamic_slice_in_dim(value_padded, row_start, block_rows + WINDOW, 0).reshape(block_rows + WINDOW, head_count, ADIM).astype(jnp.float32)
        scores = jnp.einsum('qhd,khd->hqk', query_block, key_block) * ADIM ** (-0.5)
        allowed = (col_pos > row_pos) & (col_pos <= row_pos + WINDOW) & (col_pos + row_start >= WINDOW)
        scores = jnp.where(allowed[None], scores, -1e+30)
        row_max = lax.optimization_barrier(jnp.max(scores, axis=-1, keepdims=True))
        weights = jnp.where(allowed[None], jnp.exp(scores - row_max), 0.0)
        row_total = lax.optimization_barrier(jnp.sum(weights, axis=-1, keepdims=True))
        probs_bf = (weights / row_total).astype(jnp.bfloat16)
        result = jnp.einsum('hqk,khd->qhd', probs_bf.astype(jnp.float32), value_block)
        return result.reshape(block_rows, D)
    blocks = lax.map(one_block, jnp.arange(block_count, dtype=jnp.int32))
    return blocks.reshape(TOKENS, D)

def reference(qkv, step_size, fast_in, fast_out):
    queries = qkv[0]
    key_rows = qkv[1]
    values = qkv[2]
    attended = band_attention(queries, key_rows, values)

    def by_head(array):
        return array.reshape(TOKENS, FW_HEADS, HD).transpose(1, 0, 2)
    applied = lax.map(fast_head, (by_head(queries), by_head(key_rows), by_head(values), step_size.T, fast_in, fast_out))
    applied = applied.transpose(1, 0, 2).reshape(TOKENS, D)
    return (attended + applied).astype(jnp.bfloat16)
```

```python
import math

import jax
import jax.numpy as jnp
from jax import lax
from jax.experimental import pallas as pl
from jax.experimental.pallas import tpu as pltpu
from jax.sharding import PartitionSpec as P

ADIM = 128
EPS = 1e-06
F32 = jnp.float32
BF16 = jnp.bfloat16
VMEM_LIMIT = 56 * 1024 * 1024


def call(body, grid, prefetch, in_specs, out_specs, out_shape, name, scratch=()):
    return pl.pallas_call(
        body,
        grid_spec=pltpu.PrefetchScalarGridSpec(
            num_scalar_prefetch=prefetch,
            grid=grid,
            in_specs=in_specs,
            out_specs=out_specs,
            scratch_shapes=list(scratch),
        ),
        out_shape=out_shape,
        name=name,
        compiler_params=pltpu.CompilerParams(vmem_limit_bytes=VMEM_LIMIT),
    )


def whole(shape):
    return pl.BlockSpec(shape, lambda *_: (0,) * len(shape))


def dot(a, b, dims):
    return lax.dot_general(a, b, (dims, ((), ())), preferred_element_type=F32)


def grad_parts(keys, vals, rate_rows, w_in, w_out):
    hidden_dim = w_out.shape[0]
    projected = dot(keys, w_in, ((1,), (0,)))
    gate = projected[:, :hidden_dim]
    up = projected[:, hidden_dim:]
    sig = jax.nn.sigmoid(gate)
    act = gate * sig
    slope = sig * (1.0 + gate * (1.0 - sig))
    hidden = (act * up).astype(BF16)
    rates = jnp.transpose(rate_rows)[:, :1]
    scaled = (rates * vals.astype(F32)).astype(BF16)
    back = dot(scaled, w_out, ((1,), (1,)))
    pre_gate = (back * up * slope).astype(BF16)
    pre_up = (back * act).astype(BF16)
    return hidden, scaled, pre_gate, pre_up


def grads_own(info, kv, rates, fast_in, fast_out):
    _, rows, width = kv.shape
    hidden_dim = fast_out.shape[1]

    def body(info_ref, kv_ref, rate_ref, win_ref, wout_ref, gin_ref, gout_ref):
        keys = kv_ref[0]
        hidden, scaled, pre_gate, pre_up = grad_parts(
            keys, kv_ref[1], rate_ref[...], win_ref[0], wout_ref[0]
        )
        gin_ref[:, :hidden_dim] = dot(keys, pre_gate, ((0,), (0,)))
        gin_ref[:, hidden_dim:] = dot(keys, pre_up, ((0,), (0,)))
        gout_ref[...] = dot(hidden, scaled, ((0,), (0,)))

    return call(
        body,
        (1,),
        1,
        [
            whole(kv.shape),
            whole(rates.shape),
            pl.BlockSpec((1, width, 2 * hidden_dim), lambda i, s: (s[0], 0, 0)),
            pl.BlockSpec((1, hidden_dim, width), lambda i, s: (s[0], 0, 0)),
        ],
        [whole((width, 2 * hidden_dim)), whole((hidden_dim, width))],
        [
            jax.ShapeDtypeStruct((width, 2 * hidden_dim), F32),
            jax.ShapeDtypeStruct((hidden_dim, width), F32),
        ],
        "grads_own",
    )(info, kv, rates, fast_in, fast_out)


def grads_pair(info, keys, vals, rates, fast_in, fast_out, gin, gout, in_cuts, out_cuts):
    rows, width = keys.shape
    hidden_dim = fast_out.shape[1]

    def body(info_ref, k_ref, v_ref, rate_ref, win_ref, wout_ref, gin_ref, gout_ref, *outs):
        keys_val = k_ref[...]
        hidden, scaled, pre_gate, pre_up = grad_parts(
            keys_val, v_ref[...], rate_ref[...], win_ref[0], wout_ref[0]
        )
        for (lo, hi), ref in zip(in_cuts, outs):
            size = hi - lo
            ref[:, :size] = (
                gin_ref[:, lo:hi] + dot(keys_val, pre_gate[:, lo:hi], ((0,), (0,)))
            ).astype(BF16)
            ref[:, size:] = (
                gin_ref[:, hidden_dim + lo : hidden_dim + hi]
                + dot(keys_val, pre_up[:, lo:hi], ((0,), (0,)))
            ).astype(BF16)
        for (lo, hi), ref in zip(out_cuts, outs[len(in_cuts) :]):
            ref[...] = (
                gout_ref[:, lo:hi] + dot(hidden, scaled[:, lo:hi], ((0,), (0,)))
            ).astype(BF16)

    shapes = [(width, 2 * (hi - lo)) for lo, hi in in_cuts]
    shapes += [(hidden_dim, hi - lo) for lo, hi in out_cuts]
    return call(
        body,
        (1,),
        1,
        [
            whole(keys.shape),
            whole(vals.shape),
            whole(rates.shape),
            pl.BlockSpec((1, width, 2 * hidden_dim), lambda i, s: (s[0], 0, 0)),
            pl.BlockSpec((1, hidden_dim, width), lambda i, s: (s[0], 0, 0)),
            whole(gin.shape),
            whole(gout.shape),
        ],
        [whole(s) for s in shapes],
        [jax.ShapeDtypeStruct(s, BF16) for s in shapes],
        "grads_pair",
    )(info, keys, vals, rates, fast_in, fast_out, gin, gout)


def renorm(old, update):
    moved = old + update
    old_norm = jnp.sqrt(jnp.sum(old * old, axis=0, keepdims=True))
    new_norm = jnp.sqrt(jnp.sum(moved * moved, axis=0, keepdims=True))
    return (moved * (old_norm / (new_norm + EPS))).astype(BF16)


def new_weights(info, mine, other, fast, lo, hi, factor, paired):
    _, depth, full = fast.shape
    size = hi - lo
    half = full // 2

    def body(info_ref, a_ref, b_ref, w_ref, o_ref):
        spans = [(0, lo)] + ([(size, half + lo)] if paired else [])
        for at, col in spans:
            update = a_ref[:, at : at + size].astype(F32) + b_ref[:, at : at + size].astype(F32)
            old = w_ref[0, :, col : col + size].astype(F32)
            o_ref[:, at : at + size] = renorm(old, update * factor)

    return call(
        body,
        (1,),
        1,
        [
            whole(mine.shape),
            whole(other.shape),
            pl.BlockSpec((1, depth, full), lambda i, s: (s[0], 0, 0)),
        ],
        whole(mine.shape),
        jax.ShapeDtypeStruct(mine.shape, BF16),
        "new_weights",
    )(info, mine, other, fast)


def query_hidden(info, q_own, q_oth, made, got, lo, hi):
    rows, width = q_own.shape
    size = hi - lo

    def body(info_ref, qa_ref, qb_ref, made_ref, got_ref, o_ref):
        w = jnp.where(info_ref[2] == 1, made_ref[...], got_ref[...])
        for at, ref in ((0, qa_ref), (rows, qb_ref)):
            proj = dot(ref[...], w, ((1,), (0,)))
            gate = proj[:, :size]
            o_ref[at : at + rows, :] = (gate * jax.nn.sigmoid(gate) * proj[:, size:]).astype(BF16)

    return call(
        body,
        (1,),
        1,
        [whole(q_own.shape), whole(q_oth.shape), whole(made.shape), whole(got.shape)],
        whole((2 * rows, size)),
        jax.ShapeDtypeStruct((2 * rows, size), BF16),
        "query_hidden",
    )(info, q_own, q_oth, made, got)


def apply_chunk(info, hiddens, made, got, attended, lo, hi):
    rows2 = attended.shape[0]
    rows = rows2 // 2
    size = hi - lo
    count = len(hiddens)

    def body(info_ref, *refs):
        hid = refs[:count]
        made_ref, got_ref, att_ref, own_ref, oth_ref = refs[count:]
        w = jnp.where(info_ref[2] == 1, made_ref[...], got_ref[...])
        for at, out in ((rows, oth_ref), (0, own_ref)):
            total = att_ref[at : at + rows, lo:hi]
            base = 0
            for ref in hid:
                part = ref.shape[1]
                total += dot(ref[at : at + rows, :], w[base : base + part], ((1,), (0,)))
                base += part
            out[...] = total.astype(BF16)

    return call(
        body,
        (1,),
        1,
        [whole(h.shape) for h in hiddens]
        + [whole(made.shape), whole(got.shape), whole(attended.shape)],
        [whole((rows, size))] * 2,
        [jax.ShapeDtypeStruct((rows, size), BF16)] * 2,
        "apply_chunk",
    )(info, *hiddens, made, got, attended)


def attention(info, q_own, q_oth, k_own, v_own, k_oth, v_oth, pk_own, pv_own, pk_oth, pv_oth):
    rows, width = q_own.shape
    heads = width // ADIM
    tile = min(256, rows)
    scale = ADIM ** (-0.5) * math.log2(math.e)

    def body(info_ref, qa, qb, ka, va, kb, vb, pka, pva, pkb, pvb, o_ref):
        upper = info_ref[0] == 1
        has_prev = info_ref[1] > 0
        row = lax.broadcasted_iota(jnp.int32, (tile, tile), 0)
        col = lax.broadcasted_iota(jnp.int32, (tile, tile), 1)
        causal = col <= row
        for base, q, kc, vc, kp, vp, kf1, vf1, kf0, vf0, ok1, ok0 in (
            (0, qa, ka, va, pka, pva, kb, vb, pkb, pvb, True, has_prev),
            (rows, qb, kb, vb, pkb, pvb, pka, pva, ka, va, has_prev, True),
        ):
            kf = jnp.where(upper, kf1[...], kf0[...])
            vf = jnp.where(upper, vf1[...], vf0[...])
            ok = jnp.where(upper, ok1, ok0)
            full_floor = jnp.where(ok, 0.0, -1e30)
            prev_floor = jnp.where(has_prev, 0.0, -1e30)
            for t in range(rows // tile):
                lo, hi = t * tile, (t + 1) * tile
                qt = q[lo:hi, :]
                s_cur = dot(qt, kc[0:hi, :], ((1,), (1,)))
                s_prev = dot(qt, kp[lo:, :], ((1,), (1,))) + prev_floor
                s_full = dot(qt, kf, ((1,), (1,))) + full_floor
                s_diag = jnp.where(causal, s_cur[:, lo:hi], s_prev[:, :tile])
                s_rest = [s_diag, s_full]
                if lo:
                    s_rest.append(s_cur[:, :lo])
                if hi < rows:
                    s_rest.append(s_prev[:, tile:])
                top = s_rest[0].max(axis=1, keepdims=True)
                for s in s_rest[1:]:
                    top = jnp.maximum(top, s.max(axis=1, keepdims=True))
                es = [jnp.exp2((s - top) * scale) for s in s_rest]
                total = es[0].sum(axis=1, keepdims=True)
                for e in es[1:]:
                    total += e.sum(axis=1, keepdims=True)
                e_cur = jnp.where(causal, es[0], 0.0).astype(BF16)
                e_prev = jnp.where(causal, 0.0, es[0]).astype(BF16)
                acc = dot(e_cur, vc[lo:hi, :], ((1,), (0,)))
                acc += dot(e_prev, vp[lo:hi, :], ((1,), (0,)))
                acc += dot(es[1].astype(BF16), vf, ((1,), (0,)))
                at = 2
                if lo:
                    acc += dot(es[at].astype(BF16), vc[:lo, :], ((1,), (0,)))
                    at += 1
                if hi < rows:
                    acc += dot(es[at].astype(BF16), vp[hi:, :], ((1,), (0,)))
                o_ref[base + lo : base + hi, :] = acc / total

    spec = pl.BlockSpec((rows, ADIM), lambda h, s: (0, h))
    return call(
        body,
        (heads,),
        1,
        [spec] * 10,
        pl.BlockSpec((2 * rows, ADIM), lambda h, s: (0, h)),
        jax.ShapeDtypeStruct((2 * rows, width), F32),
        "attention",
    )(info, q_own, q_oth, k_own, v_own, k_oth, v_oth, pk_own, pv_own, pk_oth, pv_oth)


def assemble(info, own_parts, oth_parts, cuts):
    rows = own_parts[0].shape[0]
    width = cuts[-1][1]
    count = len(cuts)

    def body(info_ref, *refs):
        out = refs[-1]
        keep = info_ref[0]
        for side, parts in ((keep, refs[:count]), (1 - keep, refs[count : 2 * count])):
            for (lo, hi), ref in zip(cuts, parts):
                start = pl.multiple_of(side * width + lo, 128)
                out[:, pl.ds(start, hi - lo)] = ref[...]

    return call(
        body,
        (1,),
        1,
        [whole(a.shape) for a in own_parts + oth_parts],
        whole((rows, 2 * width)),
        jax.ShapeDtypeStruct((rows, 2 * width), BF16),
        "assemble",
    )(info, *own_parts, *oth_parts)


def local(qkv, step_size, fast_in, fast_out):
    _, tok_rows, _ = qkv.shape
    head_width = fast_in.shape[1]
    hidden_dim = fast_out.shape[1]
    ctx_count = lax.axis_size("ctx")
    line = ctx_count // 2
    index = lax.axis_index("ctx").astype(jnp.int32)
    keep = index % 2
    place = index // 2
    inner = ((place == line // 2) | (place == line // 2 - 1)).astype(jnp.int32)
    info = jnp.stack([keep, place, inner])
    factor = (tok_rows * ctx_count) ** (-0.5)

    swap_pairs = [(i, i ^ 1) for i in range(ctx_count)]
    next_pairs = [(i, i + 2) for i in range(ctx_count - 2)]

    def along(moves):
        return [(2 * a + y, 2 * b + y) for a, b in moves for y in (0, 1)]

    def permute(array, pairs):
        return lax.ppermute(array, "ctx", pairs)

    def cut(which, count, side):
        return lax.dynamic_slice(
            qkv, (which, 0, side * head_width), (count, tok_rows, head_width)
        )

    away = 1 - keep
    k_oth = permute(cut(1, 1, away)[0], swap_pairs)
    v_oth = permute(cut(2, 1, away)[0], swap_pairs)
    step_rows = jnp.transpose(step_size)
    rate_own = jnp.broadcast_to(lax.dynamic_slice_in_dim(step_rows, keep, 1, 0), (8, tok_rows))
    rate_send = jnp.broadcast_to(lax.dynamic_slice_in_dim(step_rows, away, 1, 0), (8, tok_rows))
    rate_oth = permute(rate_send, swap_pairs)
    kv_own = cut(1, 2, keep)
    pkv_own = permute(kv_own, next_pairs)
    q_oth = permute(cut(0, 1, away)[0], swap_pairs)
    q_own = cut(0, 1, keep)[0]
    pk_oth = permute(k_oth, next_pairs)
    pv_oth = permute(v_oth, next_pairs)

    gin, gout = grads_own(info, kv_own, rate_own, fast_in, fast_out)
    quarter = hidden_dim // 2
    in_cuts = [(0, quarter), (quarter, 2 * quarter)]
    out_cuts = [(0, 384), (384, 640)] if head_width == 640 else [(0, head_width)]
    chunks = grads_pair(
        info, k_oth, v_oth, rate_oth, fast_in, fast_out, gin, gout, in_cuts, out_cuts
    )
    plan = [(fast_in, lo, hi, True) for lo, hi in in_cuts]
    plan += [(fast_out, lo, hi, False) for lo, hi in out_cuts]

    if line == 4:
        inward = along([(0, 1), (3, 2)])
        centre = along([(1, 2), (2, 1)])
        outward = along([(1, 0), (2, 3)])
        sums = []
        for chunk in chunks:
            got = permute(chunk, inward)
            sums.append((chunk.astype(F32) + got.astype(F32)).astype(BF16))
        made = []
        for total, (fast, lo, hi, paired) in zip(sums, plan):
            made.append(
                new_weights(info, total, permute(total, centre), fast, lo, hi, factor, paired)
            )
        got = [permute(w, outward) for w in made]
    else:
        made = []
        for chunk, (fast, lo, hi, paired) in zip(chunks, plan):
            slots = jnp.where(jnp.arange(2)[:, None, None] == keep, chunk[None].astype(F32), 0.0)
            total = lax.psum(slots, "ctx")
            total = lax.dynamic_index_in_dim(total, keep, 0, keepdims=False)
            made.append(
                new_weights(info, total, jnp.zeros_like(total), fast, lo, hi, factor, paired)
                .astype(BF16)
            )
        got = made

    attended = attention(
        info,
        q_own,
        q_oth,
        kv_own[0],
        kv_own[1],
        k_oth,
        v_oth,
        pkv_own[0],
        pkv_own[1],
        pk_oth,
        pv_oth,
    )
    hiddens = [
        query_hidden(info, q_own, q_oth, made[i], got[i], lo, hi)
        for i, (lo, hi) in enumerate(in_cuts)
    ]
    own_parts, oth_parts = [], []
    for i, (lo, hi) in enumerate(out_cuts):
        at = len(in_cuts) + i
        mine, theirs = apply_chunk(info, hiddens, made[at], got[at], attended, lo, hi)
        own_parts.append(mine)
        oth_parts.append(permute(theirs, swap_pairs))
    return assemble(info, own_parts, oth_parts, out_cuts)


def solution(mesh):
    placed = (
        P(None, "ctx", "head"),
        P("ctx", "head"),
        P("head", None, None),
        P("head", None, None),
    )
    return jax.shard_map(
        local, mesh=mesh, in_specs=placed, out_specs=P("ctx", "head"), check_vma=False
    )
```

```python
import math

import jax
import jax.numpy as jnp
from jax import lax
from jax.experimental import pallas as pl
from jax.experimental.pallas import tpu as pltpu
from jax.sharding import PartitionSpec as P


ADIM = 128
EPS = 1e-06
F32 = jnp.float32
BF16 = jnp.bfloat16
PIECES = 4
VMEM_LIMIT = 20 * 1024 * 1024


VM = pl.BlockSpec(memory_space=pltpu.VMEM)
SM = pl.BlockSpec(memory_space=pltpu.SMEM)
HBM = pl.BlockSpec(memory_space=pltpu.HBM)


def sds(shape, dtype):
    return jax.ShapeDtypeStruct(shape, dtype)


def call(body, ins, outs, args, out_specs=None, scratch=()):
    return pl.pallas_call(
        body,
        in_specs=ins,
        out_specs=out_specs if out_specs is not None else [VM] * len(outs),
        out_shape=outs,
        scratch_shapes=list(scratch),
        compiler_params=pltpu.CompilerParams(vmem_limit_bytes=VMEM_LIMIT),
    )(*args)


def dot(a, b, dims):
    return lax.dot_general(a, b, (dims, ((), ())), preferred_element_type=F32)


def cut_blocks(info, qkv, picks, width):
    rows = qkv.shape[1]
    count = len(picks)

    def body(info_ref, qkv_ref, *rest):
        outs, sem = rest[:count], rest[count]
        copies = []
        for at, (which, own) in enumerate(picks):
            side = info_ref[0] if own else 1 - info_ref[0]
            cols = pl.ds(pl.multiple_of(side * width, ADIM), width)
            for piece in range(PIECES):
                some = pl.ds(piece * (rows // PIECES), rows // PIECES)
                copies.append(
                    pltpu.make_async_copy(
                        qkv_ref.at[which, some, cols], outs[at].at[some, :], sem.at[at, piece]
                    )
                )
        for copy in copies:
            copy.start()
        for copy in copies:
            copy.wait()

    return call(
        body,
        [SM, HBM],
        [sds((rows, width), BF16)] * count,
        (info, qkv),
        scratch=[pltpu.SemaphoreType.DMA((count, PIECES))],
    )


def stack_columns(arrays, cuts):
    count = len(arrays)

    def body(*refs):
        for (lo, hi), out in zip(cuts, refs[count:]):
            for at, ref in enumerate(refs[:count]):
                out[at] = ref[:, lo:hi]

    shapes = [(count, arrays[0].shape[0], hi - lo) for lo, hi in cuts]
    return call(body, [VM] * count, [sds(shape, BF16) for shape in shapes], arrays)


def gate_parts(keys, w_in, hidden_dim):
    projected = dot(keys, w_in, ((1,), (0,)))
    gate = projected[:, :hidden_dim]
    up = projected[:, hidden_dim:]
    sig = jax.nn.sigmoid(gate)
    act = gate * sig
    slope = sig * (1.0 + gate * (1.0 - sig))
    return (act * up).astype(BF16), up * slope, act


def scale_rows(vals, rate_rows):
    return (jnp.transpose(rate_rows)[:, :1] * vals.astype(F32)).astype(BF16)


def back_parts(scaled, w_out, tilt, act):
    back = dot(scaled, w_out, ((1,), (1,)))
    return (back * tilt).astype(BF16), (back * act).astype(BF16)


def grads_own(info, keys, vals, rates, fast_in, fast_out):
    width = keys.shape[1]
    hidden_dim = fast_out.shape[1]

    def body(info_ref, k_ref, v_ref, rate_ref, win_ref, wout_ref, gin_ref, gout_ref):
        keep = info_ref[0]
        hidden, tilt, act = gate_parts(k_ref[...], win_ref[keep], hidden_dim)
        scaled = scale_rows(v_ref[...], rate_ref[...])
        pre_gate, pre_up = back_parts(scaled, wout_ref[keep], tilt, act)
        gin_ref[:, :hidden_dim] = dot(k_ref[...], pre_gate, ((0,), (0,)))
        gin_ref[:, hidden_dim:] = dot(k_ref[...], pre_up, ((0,), (0,)))
        gout_ref[...] = dot(hidden, scaled, ((0,), (0,)))

    return call(
        body,
        [SM] + [VM] * 5,
        [sds((width, 2 * hidden_dim), F32), sds((hidden_dim, width), F32)],
        (info, keys, vals, rates, fast_in, fast_out),
    )


def pair_gates(info, keys, fast_in, hidden_dim):
    rows = keys.shape[0]

    def body(info_ref, k_ref, win_ref, hid_ref, tilt_ref, act_ref):
        hidden, tilt, act = gate_parts(k_ref[...], win_ref[info_ref[0]], hidden_dim)
        hid_ref[...] = hidden
        tilt_ref[...] = tilt
        act_ref[...] = act

    shape = (rows, hidden_dim)
    return call(
        body,
        [SM, VM, VM],
        [sds(shape, BF16), sds(shape, F32), sds(shape, F32)],
        (info, keys, fast_in),
    )


def pair_first(hidden, vals, rates, gout, lo, hi):
    def body(h_ref, v_ref, rate_ref, gout_ref, scaled_ref, send_ref, kept_ref):
        scaled = scale_rows(v_ref[...], rate_ref[...])
        scaled_ref[...] = scaled
        part = gout_ref[:, lo:hi] + dot(h_ref[...], scaled[:, lo:hi], ((0,), (0,)))
        send_ref[...] = part.astype(BF16)
        kept_ref[...] = part

    shape = (gout.shape[0], hi - lo)
    return call(
        body,
        [VM] * 4,
        [sds(vals.shape, BF16), sds(shape, BF16), sds(shape, F32)],
        (hidden, vals, rates, gout),
    )


def pair_grads(info, keys, scaled, fast_out, gates, gin, gout, in_cuts, out_cuts):
    width = keys.shape[1]
    hidden_dim = fast_out.shape[1]
    count = len(in_cuts) + len(out_cuts)

    def body(info_ref, k_ref, s_ref, wout_ref, h_ref, t_ref, a_ref, gin_ref, gout_ref, *o):
        pre_gate, pre_up = back_parts(s_ref[...], wout_ref[info_ref[0]], t_ref[...], a_ref[...])
        for at, (lo, hi) in enumerate(in_cuts):
            size = hi - lo
            for start, base, pre in ((0, lo, pre_gate), (size, hidden_dim + lo, pre_up)):
                part = gin_ref[:, base : base + size]
                part += dot(k_ref[...], pre[:, lo:hi], ((0,), (0,)))
                o[at][:, start : start + size] = part.astype(BF16)
                o[count + at][:, start : start + size] = part
        for at, (lo, hi) in enumerate(out_cuts, len(in_cuts)):
            part = gout_ref[:, lo:hi] + dot(h_ref[...], s_ref[:, lo:hi], ((0,), (0,)))
            o[at][...] = part.astype(BF16)
            o[count + at][...] = part

    shapes = [(width, 2 * (hi - lo)) for lo, hi in in_cuts]
    shapes += [(hidden_dim, hi - lo) for lo, hi in out_cuts]
    outs = call(
        body,
        [SM] + [VM] * 8,
        [sds(s, BF16) for s in shapes] + [sds(s, F32) for s in shapes],
        (info, keys, scaled, fast_out, *gates, gin, gout),
    )
    return outs[:count], outs[count:]


def add_chunk(kept, got):
    def body(kept_ref, got_ref, send_ref, sum_ref):
        total = kept_ref[...] + got_ref[...].astype(F32)
        send_ref[...] = total.astype(BF16)
        sum_ref[...] = total

    return call(body, [VM] * 2, [sds(kept.shape, BF16), sds(kept.shape, F32)], (kept, got))


def new_weights(info, mine, others, fast, lo, hi, factor, paired):
    count = len(others)
    size = hi - lo
    half = fast.shape[2] // 2

    def body(info_ref, a_ref, *rest):
        w_ref, o_ref = rest[count:]
        keep = info_ref[0]
        spans = [(0, lo)] + ([(size, half + lo)] if paired else [])
        for start, col in spans:
            total = a_ref[:, start : start + size]
            for b_ref in rest[:count]:
                total += b_ref[:, start : start + size].astype(F32)
            old = w_ref[keep, :, col : col + size].astype(F32)
            moved = old + total * factor
            old_norm = jnp.sqrt(jnp.sum(old * old, axis=0, keepdims=True))
            new_norm = jnp.sqrt(jnp.sum(moved * moved, axis=0, keepdims=True))
            o_ref[:, start : start + size] = (moved * (old_norm / (new_norm + EPS))).astype(BF16)

    return call(
        body, [SM] + [VM] * (count + 2), [sds(mine.shape, BF16)], (info, mine, *others, fast)
    )[0]


def query_hidden(info, q_own, q_oth, made, got):
    rows = q_own.shape[0]
    size = made.shape[1] // 2

    def body(info_ref, qa_ref, qb_ref, made_ref, got_ref, o_ref):
        def run(w_ref):
            for start, ref in ((0, qa_ref), (rows, qb_ref)):
                proj = dot(ref[...], w_ref[...], ((1,), (0,)))
                gate = proj[:, :size]
                o_ref[start : start + rows, :] = (
                    gate * jax.nn.sigmoid(gate) * proj[:, size:]
                ).astype(BF16)

        @pl.when(info_ref[2] == 1)
        def _():
            run(made_ref)

        @pl.when(info_ref[2] != 1)
        def _():
            run(got_ref)

    return call(
        body, [SM] + [VM] * 4, [sds((2 * rows, size), BF16)], (info, q_own, q_oth, made, got)
    )[0]


def apply_chunk(info, hiddens, made, got, parts, late, lo, hi):
    rows = hiddens[0].shape[0] // 2
    size = hi - lo
    count = len(hiddens)
    (own_sum, own_at, own_p), (oth_sum, oth_at, oth_p) = parts
    vals = [array for group in late for array, _, _ in group]

    def body(info_ref, *refs):
        hid = refs[:count]
        made_ref, got_ref = refs[count : count + 2]
        val_refs = list(refs[count + 2 : count + 2 + len(vals)])
        att = refs[count + 2 + len(vals) : -2]
        own_ref, oth_ref = refs[-2:]
        groups = [[(val_refs.pop(0), *place) for _, *place in group] for group in late]

        def values(group, head):
            total = None
            for ref, base, layer_at in group:
                col = lo - base + head * ADIM
                cols = slice(col, col + ADIM)
                piece = ref[:, cols] if layer_at is None else ref[layer_at, :, cols]
                total = piece if total is None else total + piece
            return total

        def run(w_ref):
            for start, out, sum_ref, base, p_ref, order in (
                (rows, oth_ref, att[2], oth_at, att[3], (1, 0)),
                (0, own_ref, att[0], own_at, att[1], (0, 1)),
            ):
                total = sum_ref[:, base : base + size]
                row = 0
                for ref in hid:
                    part = ref.shape[1]
                    total += dot(
                        ref[start : start + rows, :], w_ref[row : row + part, :], ((1,), (0,))
                    )
                    row += part
                for head in range(size // ADIM):
                    col = head * ADIM
                    mixed = total[:, col : col + ADIM]
                    for place, which in enumerate(order):
                        p = p_ref[base // ADIM + head, :, place * rows : (place + 1) * rows]
                        v = values(groups[which], head)
                        if place == 1:
                            v = jnp.where(info_ref[0] == which, jnp.zeros_like(v), v)
                        mixed += dot(p, v, ((1,), (0,)))
                    out[:, col : col + ADIM] = mixed.astype(BF16)

        @pl.when(info_ref[2] == 1)
        def _():
            run(made_ref)

        @pl.when(info_ref[2] != 1)
        def _():
            run(got_ref)

    return call(
        body,
        [SM] + [VM] * (count + 2 + len(vals) + 4),
        [sds((rows, size), BF16)] * 2,
        (info, *hiddens, made, got, *vals, own_sum, own_p, oth_sum, oth_p),
    )


def attention(info, side, heads, q, k_own, v_own, k_oth, v_oth, pk_own, pk_oth):
    rows = q.shape[0]
    tile = min(256, rows)
    first, last = heads
    number = last - first
    scale = ADIM ** (-0.5) * math.log2(math.e)
    if side == 0:
        arrays = (q, k_own, v_own, pk_own, k_oth, v_oth, pk_oth)
    else:
        arrays = (q, k_oth, v_oth, pk_oth, k_own, v_own, pk_own)

    def body(info_ref, q_ref, kc, vc, kp, k_pair, v_pair, k_before, o_ref, p_ref, kf, vf):
        has_prev = info_ref[1] > 0
        in_pair = info_ref[0] == 1 - side
        row = lax.broadcasted_iota(jnp.int32, (tile, tile), 0)
        col = lax.broadcasted_iota(jnp.int32, (tile, tile), 1)
        causal = col <= row
        prev_floor = jnp.where(has_prev, 0.0, -1e30)
        full_floor = jnp.where(jnp.logical_or(in_pair, has_prev), 0.0, -1e30)

        def one_head(at, carry):
            cols = pl.ds(pl.multiple_of((first + at) * ADIM, ADIM), ADIM)
            outs = pl.ds(pl.multiple_of(at * ADIM, ADIM), ADIM)

            @pl.when(in_pair)
            def _():
                kf[...] = k_pair[:, cols]
                vf[...] = v_pair[:, cols]

            @pl.when(jnp.logical_not(in_pair))
            def _():
                kf[...] = k_before[:, cols]
                vf[...] = jnp.zeros_like(vf)

            for t in range(rows // tile):
                lo, hi = t * tile, (t + 1) * tile
                qt = q_ref[lo:hi, cols]
                s_cur = dot(qt, kc[0:hi, cols], ((1,), (1,)))
                s_prev = dot(qt, kp[lo:, cols], ((1,), (1,))) + prev_floor
                s_full = dot(qt, kf[...], ((1,), (1,))) + full_floor
                s_rest = [jnp.where(causal, s_cur[:, lo:hi], s_prev[:, :tile]), s_full]
                if lo:
                    s_rest.append(s_cur[:, :lo])
                if hi < rows:
                    s_rest.append(s_prev[:, tile:])
                top = s_rest[0].max(axis=1, keepdims=True)
                for s in s_rest[1:]:
                    top = jnp.maximum(top, s.max(axis=1, keepdims=True))
                es = [jnp.exp2((s - top) * scale) for s in s_rest]
                total = es[0].sum(axis=1, keepdims=True)
                for e in es[1:]:
                    total += e.sum(axis=1, keepdims=True)
                share = 1.0 / total
                e_cur = jnp.where(causal, es[0], 0.0).astype(BF16)
                acc = dot(e_cur, vc[lo:hi, cols], ((1,), (0,)))
                acc += dot(es[1].astype(BF16), vf[...], ((1,), (0,)))
                if lo:
                    acc += dot(es[2].astype(BF16), vc[:lo, cols], ((1,), (0,)))
                    p_ref[at, lo:hi, :lo] = jnp.zeros((tile, lo), BF16)
                p_ref[at, lo:hi, lo:hi] = jnp.where(causal, 0.0, es[0] * share).astype(BF16)
                if hi < rows:
                    p_ref[at, lo:hi, hi:rows] = (es[-1] * share).astype(BF16)
                p_ref[at, lo:hi, rows:] = (es[1] * share).astype(BF16)
                o_ref[lo:hi, outs] = acc * share
            return carry

        lax.fori_loop(0, number, one_head, 0)

    return call(
        body,
        [SM] + [VM] * 7,
        [sds((rows, number * ADIM), F32), sds((number, rows, 2 * rows), BF16)],
        (info, *arrays),
        scratch=[pltpu.VMEM((rows, ADIM), BF16)] * 2,
    )


def assemble(info, own_parts, oth_parts, cuts):
    rows = own_parts[0].shape[0]
    width = cuts[-1][1]
    count = len(cuts)

    def body(info_ref, *refs):
        parts, out, sem = refs[: 2 * count], refs[2 * count], refs[2 * count + 1]
        copies = []
        for at, ref in enumerate(parts):
            side = info_ref[0] if at < count else 1 - info_ref[0]
            lo, hi = cuts[at % count]
            start = pl.multiple_of(side * width + lo, ADIM)
            copies.append(
                pltpu.make_async_copy(ref, out.at[:, pl.ds(start, hi - lo)], sem.at[at])
            )
        for copy in copies:
            copy.start()
        for copy in copies:
            copy.wait()

    return call(
        body,
        [SM] + [VM] * (2 * count),
        [sds((rows, 2 * width), BF16)],
        (info, *own_parts, *oth_parts),
        out_specs=[HBM],
        scratch=[pltpu.SemaphoreType.DMA((2 * count,))],
    )[0]


def rate_rows(info, step_size):
    rows = step_size.shape[0]

    def body(info_ref, step_ref, own_ref, send_ref):
        both = jnp.transpose(step_ref[...])
        upper = info_ref[0] == 1
        own_ref[...] = jnp.broadcast_to(jnp.where(upper, both[1:2], both[0:1]), (8, rows))
        send_ref[...] = jnp.broadcast_to(jnp.where(upper, both[0:1], both[1:2]), (8, rows))

    return call(body, [SM, VM], [sds((8, rows), F32)] * 2, (info, step_size))


def layer(qkv, step_size, fast_in, fast_out):
    _, tok_rows, _ = qkv.shape
    head_width = fast_in.shape[1]
    hidden_dim = fast_out.shape[1]
    ctx_count = lax.axis_size("ctx")
    line = ctx_count // 2
    index = lax.axis_index("ctx").astype(jnp.int32)
    keep = index % 2
    place = index // 2
    inner = ((place == line // 2) | (place == line // 2 - 1)).astype(jnp.int32)
    info = jnp.stack([keep, place, inner])
    factor = (tok_rows * ctx_count) ** (-0.5)

    swap_pairs = [(i, i ^ 1) for i in range(ctx_count)]
    next_pairs = [(i, i + 2) for i in range(ctx_count - 2)]

    def along(moves):
        return [(2 * a + y, 2 * b + y) for a, b in moves for y in (0, 1)]

    def permute(array, pairs):
        return lax.ppermute(array, "ctx", pairs)

    parts = 4
    part = hidden_dim // parts
    in_cuts = [(i * part, (i + 1) * part) for i in range(parts)]
    middle = (head_width // ADIM + 1) // 2 * ADIM
    out_cuts = [(0, middle), (middle, head_width)]

    qkv = pltpu.with_memory_space_constraint(qkv, pltpu.HBM)
    k_away, k_own = cut_blocks(info, qkv, [(1, False), (1, True)], head_width)
    k_oth = permute(k_away, swap_pairs)
    pk_own = permute(k_own, next_pairs)
    v_away, v_own = cut_blocks(info, qkv, [(2, False), (2, True)], head_width)
    rate_own, rate_send = rate_rows(info, step_size)
    rate_oth = permute(rate_send, swap_pairs)
    v_oth = permute(v_away, swap_pairs)
    q_away, q_own = cut_blocks(info, qkv, [(0, False), (0, True)], head_width)
    q_oth = permute(q_away, swap_pairs)
    pk_oth = permute(k_oth, next_pairs)
    if line == 4:
        own_early = permute(v_own, along([(1, 2), (2, 3)]))
        oth_early = permute(v_oth, along([(2, 3)]))
        stacks = stack_columns((v_own, v_oth), out_cuts)
        singles = stack_columns((v_oth,), out_cuts)
        late_vals = []
        for i, (lo, hi) in enumerate(out_cuts):
            first = permute(stacks[i], along([(0, 1)]))
            second = permute(singles[i], along([(1, 2)]))
            late_vals.append((
                [(own_early, 0, None), (first, lo, 0)],
                [(oth_early, 0, None), (first, lo, 1), (second, lo, 0)],
            ))
    else:
        late_vals = [(
            [(permute(v_own, next_pairs), 0, None)], [(permute(v_oth, next_pairs), 0, None)]
        )] * len(out_cuts)

    gin, gout = grads_own(info, k_own, v_own, rate_own, fast_in, fast_out)
    gates = pair_gates(info, k_oth, fast_in, hidden_dim)
    scaled, *first = pair_first(gates[0], v_oth, rate_oth, gout, *out_cuts[0])
    send, kept = pair_grads(
        info, k_oth, scaled, fast_out, gates, gin, gout, in_cuts, out_cuts[1:]
    )
    send, kept = [first[0], *send], [first[1], *kept]
    plan = [(fast_out, *out_cuts[0], False)]
    plan += [(fast_in, lo, hi, True) for lo, hi in in_cuts]
    plan += [(fast_out, lo, hi, False) for lo, hi in out_cuts[1:]]

    made, got = [], []
    if line == 4:
        inward = along([(0, 1), (3, 2)])
        centre = along([(1, 2), (2, 1)])
        outward = along([(1, 0), (2, 3)])
        for at, (fast, lo, hi, paired) in enumerate(plan):
            half_sum, total = add_chunk(kept[at], permute(send[at], inward))
            crossed = [permute(half_sum, centre)]
            made.append(new_weights(info, total, crossed, fast, lo, hi, factor, paired))
            got.append(permute(made[at], outward))
    else:
        for at, (fast, lo, hi, paired) in enumerate(plan):
            slots = jnp.where(jnp.arange(2)[:, None, None] == keep, kept[at][None], 0.0)
            total = lax.dynamic_index_in_dim(lax.psum(slots, "ctx"), keep, 0, keepdims=False)
            made.append(new_weights(info, total, (), fast, lo, hi, factor, paired))
        got = made

    heads = head_width // ADIM
    split = middle // ADIM
    blocks = (k_own, v_own, k_oth, v_oth, pk_own, pk_oth)
    own_sum, own_p = attention(info, 0, (0, heads), q_own, *blocks)
    oth_some = attention(info, 1, (0, split), q_oth, *blocks)
    oth_rest = attention(info, 1, (split, heads), q_oth, *blocks)
    hiddens = [query_hidden(info, q_own, q_oth, made[i], got[i]) for i in range(1, 1 + parts)]
    own_parts, oth_parts = [], []
    for i, (lo, hi) in enumerate(out_cuts):
        at = parts + i if i else 0
        left = (own_sum, lo, own_p), (
            (oth_some[0], lo, oth_some[1]) if lo < middle else (oth_rest[0], lo - middle, oth_rest[1])
        )
        mine, theirs = apply_chunk(info, hiddens, made[at], got[at], left, late_vals[i], lo, hi)
        own_parts.append(mine)
        oth_parts.append(permute(theirs, swap_pairs))
    return assemble(info, own_parts, oth_parts, out_cuts)


def solution(mesh):
    placed = (
        P(None, "ctx", "head"),
        P("ctx", "head"),
        P("head", None, None),
        P("head", None, None),
    )
    return jax.shard_map(
        layer, mesh=mesh, in_specs=placed, out_specs=P("ctx", "head"), check_vma=False
    )
```

```python
import math

import jax
import jax.numpy as jnp
from jax import lax
from jax.experimental import pallas as pl
from jax.experimental.pallas import tpu as pltpu
from jax.sharding import PartitionSpec as P


ADIM = 128
EPS = 1e-06
F32 = jnp.float32
BF16 = jnp.bfloat16
PIECES = 4
VMEM_LIMIT = 20 * 1024 * 1024


VM = pl.BlockSpec(memory_space=pltpu.VMEM)
SM = pl.BlockSpec(memory_space=pltpu.SMEM)
HBM = pl.BlockSpec(memory_space=pltpu.HBM)


def sds(shape, dtype):
    return jax.ShapeDtypeStruct(shape, dtype)


def call(body, ins, outs, args, out_specs=None, scratch=()):
    return pl.pallas_call(
        body,
        in_specs=ins,
        out_specs=out_specs if out_specs is not None else [VM] * len(outs),
        out_shape=outs,
        scratch_shapes=list(scratch),
        compiler_params=pltpu.CompilerParams(vmem_limit_bytes=VMEM_LIMIT),
    )(*args)


def dot(a, b, dims):
    return lax.dot_general(a, b, (dims, ((), ())), preferred_element_type=F32)


def cut_blocks(info, qkv, picks, width):
    rows = qkv.shape[1]
    count = len(picks)

    def body(info_ref, qkv_ref, *rest):
        outs, sem = rest[:count], rest[count]
        copies = []
        for at, (which, own) in enumerate(picks):
            side = info_ref[0] if own else 1 - info_ref[0]
            cols = pl.ds(pl.multiple_of(side * width, ADIM), width)
            for piece in range(PIECES):
                some = pl.ds(piece * (rows // PIECES), rows // PIECES)
                copies.append(
                    pltpu.make_async_copy(
                        qkv_ref.at[which, some, cols], outs[at].at[some, :], sem.at[at, piece]
                    )
                )
        for copy in copies:
            copy.start()
        for copy in copies:
            copy.wait()

    return call(
        body,
        [SM, HBM],
        [sds((rows, width), BF16)] * count,
        (info, qkv),
        scratch=[pltpu.SemaphoreType.DMA((count, PIECES))],
    )


def late_columns(first, second, cuts):
    count = len(cuts)

    def body(a_ref, b_ref, *outs):
        for (lo, hi), stack, single in zip(cuts, outs, outs[count:]):
            stack[0] = a_ref[:, lo:hi]
            stack[1] = b_ref[:, lo:hi]
            single[...] = b_ref[:, lo:hi]

    rows = first.shape[0]
    shapes = [(2, rows, hi - lo) for lo, hi in cuts] + [(rows, hi - lo) for lo, hi in cuts]
    outs = call(body, [VM] * 2, [sds(shape, BF16) for shape in shapes], (first, second))
    return outs[:count], outs[count:]


def gate_parts(keys, w_in, hidden_dim):
    projected = dot(keys, w_in, ((1,), (0,)))
    gate = projected[:, :hidden_dim]
    up = projected[:, hidden_dim:]
    sig = jax.nn.sigmoid(gate)
    act = gate * sig
    slope = sig * (1.0 + gate * (1.0 - sig))
    return (act * up).astype(BF16), up * slope, act


def scale_rows(vals, rate_rows):
    return (jnp.transpose(rate_rows)[:, :1] * vals.astype(F32)).astype(BF16)


def back_parts(scaled, w_out, tilt, act):
    back = dot(scaled, w_out, ((1,), (1,)))
    return (back * tilt).astype(BF16), (back * act).astype(BF16)


def grads_own(info, keys, vals, rates, fast_in, fast_out):
    width = keys.shape[1]
    hidden_dim = fast_out.shape[1]

    def body(info_ref, k_ref, v_ref, rate_ref, win_ref, wout_ref, gin_ref, gout_ref):
        keep = info_ref[0]
        hidden, tilt, act = gate_parts(k_ref[...], win_ref[keep], hidden_dim)
        scaled = scale_rows(v_ref[...], rate_ref[...])
        pre_gate, pre_up = back_parts(scaled, wout_ref[keep], tilt, act)
        gin_ref[:, :hidden_dim] = dot(k_ref[...], pre_gate, ((0,), (0,)))
        gin_ref[:, hidden_dim:] = dot(k_ref[...], pre_up, ((0,), (0,)))
        gout_ref[...] = dot(hidden, scaled, ((0,), (0,)))

    return call(
        body,
        [SM] + [VM] * 5,
        [sds((width, 2 * hidden_dim), F32), sds((hidden_dim, width), F32)],
        (info, keys, vals, rates, fast_in, fast_out),
    )


def pair_gates(info, keys, fast_in, hidden_dim):
    rows = keys.shape[0]

    def body(info_ref, k_ref, win_ref, hid_ref, tilt_ref, act_ref):
        hidden, tilt, act = gate_parts(k_ref[...], win_ref[info_ref[0]], hidden_dim)
        hid_ref[...] = hidden
        tilt_ref[...] = tilt
        act_ref[...] = act

    shape = (rows, hidden_dim)
    return call(
        body,
        [SM, VM, VM],
        [sds(shape, BF16), sds(shape, F32), sds(shape, F32)],
        (info, keys, fast_in),
    )


def pair_first(hidden, vals, rates, gout, lo, hi):
    def body(h_ref, v_ref, rate_ref, gout_ref, scaled_ref, send_ref, kept_ref):
        scaled = scale_rows(v_ref[...], rate_ref[...])
        scaled_ref[...] = scaled
        part = gout_ref[:, lo:hi] + dot(h_ref[...], scaled[:, lo:hi], ((0,), (0,)))
        send_ref[...] = part.astype(BF16)
        kept_ref[...] = part

    shape = (gout.shape[0], hi - lo)
    return call(
        body,
        [VM] * 4,
        [sds(vals.shape, BF16), sds(shape, BF16), sds(shape, F32)],
        (hidden, vals, rates, gout),
    )


def pair_grads(info, keys, scaled, fast_out, gates, gin, gout, in_cuts, out_cuts):
    width = keys.shape[1]
    hidden_dim = fast_out.shape[1]
    count = len(in_cuts) + len(out_cuts)

    def body(info_ref, k_ref, s_ref, wout_ref, h_ref, t_ref, a_ref, gin_ref, gout_ref, *o):
        sends = [o[i] for i in range(count - 2)]
        sends += [o[count - 2].at[:width, :], o[count - 2].at[width:, :]]
        keeps = o[count - 1 :]
        pre_gate, pre_up = back_parts(s_ref[...], wout_ref[info_ref[0]], t_ref[...], a_ref[...])
        for at, (lo, hi) in enumerate(in_cuts):
            size = hi - lo
            for start, base, pre in ((0, lo, pre_gate), (size, hidden_dim + lo, pre_up)):
                part = gin_ref[:, base : base + size]
                part += dot(k_ref[...], pre[:, lo:hi], ((0,), (0,)))
                sends[at][:, start : start + size] = part.astype(BF16)
                keeps[at][:, start : start + size] = part
        for at, (lo, hi) in enumerate(out_cuts, len(in_cuts)):
            part = gout_ref[:, lo:hi] + dot(h_ref[...], s_ref[:, lo:hi], ((0,), (0,)))
            sends[at][...] = part.astype(BF16)
            keeps[at][...] = part

    shapes = [(width, 2 * (hi - lo)) for lo, hi in in_cuts]
    shapes += [(hidden_dim, hi - lo) for lo, hi in out_cuts]
    joined = (shapes[-2][0] + shapes[-1][0], shapes[-1][1])
    outs = call(
        body,
        [SM] + [VM] * 8,
        [sds(s, BF16) for s in shapes[:-2] + [joined]] + [sds(s, F32) for s in shapes],
        (info, keys, scaled, fast_out, *gates, gin, gout),
    )
    return outs[: count - 1], outs[count - 1 :]


def add_chunk(kept, got, first):
    rows = kept.shape[0]

    def body(kept_ref, got_ref, send_ref, sum_ref):
        total = kept_ref[...] + got_ref[first : first + rows, :].astype(F32)
        send_ref[...] = total.astype(BF16)
        sum_ref[...] = total

    return call(body, [VM] * 2, [sds(kept.shape, BF16), sds(kept.shape, F32)], (kept, got))


def column_norms(info, fast_in, fast_out):
    def body(info_ref, win_ref, wout_ref, in_ref, out_ref):
        for ref, out in ((win_ref, in_ref), (wout_ref, out_ref)):
            old = ref[info_ref[0]].astype(F32)
            out[...] = jnp.sqrt(jnp.sum(old * old, axis=0, keepdims=True))

    return call(
        body,
        [SM, VM, VM],
        [sds((1, fast_in.shape[2]), F32), sds((1, fast_out.shape[2]), F32)],
        (info, fast_in, fast_out),
    )


def new_weights(info, mine, others, fast, norms, lo, hi, factor, paired):
    count = len(others)
    size = hi - lo
    half = fast.shape[2] // 2

    def body(info_ref, a_ref, *rest):
        w_ref, norm_ref, o_ref = rest[count:]
        keep = info_ref[0]
        spans = [(0, lo)] + ([(size, half + lo)] if paired else [])
        for start, col in spans:
            total = a_ref[:, start : start + size]
            for b_ref in rest[:count]:
                total += b_ref[:, start : start + size].astype(F32)
            moved = w_ref[keep, :, col : col + size].astype(F32) + total * factor
            new_norm = jnp.sqrt(jnp.sum(moved * moved, axis=0, keepdims=True))
            ratio = norm_ref[:, col : col + size] / (new_norm + EPS)
            o_ref[:, start : start + size] = (moved * ratio).astype(BF16)

    return call(
        body, [SM] + [VM] * (count + 3), [sds(mine.shape, BF16)], (info, mine, *others, fast, norms)
    )[0]


def query_hidden(info, q_own, q_oth, made, got):
    rows = q_own.shape[0]
    size = made.shape[1] // 2

    def body(info_ref, qa_ref, qb_ref, made_ref, got_ref, o_ref):
        def run(w_ref):
            for start, ref in ((0, qa_ref), (rows, qb_ref)):
                proj = dot(ref[...], w_ref[...], ((1,), (0,)))
                gate = proj[:, :size]
                o_ref[start : start + rows, :] = (
                    gate * jax.nn.sigmoid(gate) * proj[:, size:]
                ).astype(BF16)

        @pl.when(info_ref[2] == 1)
        def _():
            run(made_ref)

        @pl.when(info_ref[2] != 1)
        def _():
            run(got_ref)

    return call(
        body, [SM] + [VM] * 4, [sds((2 * rows, size), BF16)], (info, q_own, q_oth, made, got)
    )[0]


def apply_chunk(info, side, hiddens, made, got, left, late, lo, hi):
    rows = hiddens[0].shape[0] // 2
    size = hi - lo
    count = len(hiddens)
    sums, base, weights = left
    vals = [array for group in late for array, _, _ in group]

    def body(info_ref, *refs):
        hid = refs[:count]
        made_ref, got_ref = refs[count : count + 2]
        val_refs = list(refs[count + 2 : count + 2 + len(vals)])
        sum_ref, p_ref, out = refs[-3:]
        groups = [[(val_refs.pop(0), *place) for _, *place in group] for group in late]

        def values(group, head):
            total = None
            for ref, first, layer_at in group:
                col = lo - first + head * ADIM
                cols = slice(col, col + ADIM)
                piece = ref[:, cols] if layer_at is None else ref[layer_at, :, cols]
                total = piece if total is None else total + piece
            return total

        def run(w_ref):
            total = sum_ref[:, base : base + size]
            row = 0
            for ref in hid:
                part = ref.shape[1]
                total += dot(
                    ref[side * rows : (side + 1) * rows, :], w_ref[row : row + part, :], ((1,), (0,))
                )
                row += part
            for head in range(size // ADIM):
                col = head * ADIM
                mixed = total[:, col : col + ADIM]
                for place, which in enumerate((side, 1 - side)):
                    p = p_ref[base // ADIM + head, :, place * rows : (place + 1) * rows]
                    v = values(groups[which], head)
                    if place == 1:
                        v = jnp.where(info_ref[0] == which, jnp.zeros_like(v), v)
                    mixed += dot(p, v, ((1,), (0,)))
                out[:, col : col + ADIM] = mixed.astype(BF16)

        @pl.when(info_ref[2] == 1)
        def _():
            run(made_ref)

        @pl.when(info_ref[2] != 1)
        def _():
            run(got_ref)

    return call(
        body,
        [SM] + [VM] * (count + 2 + len(vals) + 2),
        [sds((rows, size), BF16)],
        (info, *hiddens, made, got, *vals, sums, weights),
    )[0]


def attention(info, side, heads, q, k_own, v_own, k_oth, v_oth, pk_own, pk_oth):
    rows = q.shape[0]
    tile = min(256, rows)
    first, last = heads
    number = last - first
    scale = ADIM ** (-0.5) * math.log2(math.e)
    if side == 0:
        arrays = (q, k_own, v_own, pk_own, k_oth, v_oth, pk_oth)
    else:
        arrays = (q, k_oth, v_oth, pk_oth, k_own, v_own, pk_own)

    def body(info_ref, q_ref, kc, vc, kp, k_pair, v_pair, k_before, o_ref, p_ref, kf, vf):
        has_prev = info_ref[1] > 0
        in_pair = info_ref[0] == 1 - side
        row = lax.broadcasted_iota(jnp.int32, (tile, tile), 0)
        col = lax.broadcasted_iota(jnp.int32, (tile, tile), 1)
        causal = col <= row
        prev_floor = jnp.where(has_prev, 0.0, -1e30)
        full_floor = jnp.where(jnp.logical_or(in_pair, has_prev), 0.0, -1e30)

        def one_head(at, carry):
            cols = pl.ds(pl.multiple_of((first + at) * ADIM, ADIM), ADIM)
            outs = pl.ds(pl.multiple_of(at * ADIM, ADIM), ADIM)

            @pl.when(in_pair)
            def _():
                kf[...] = k_pair[:, cols]
                vf[...] = v_pair[:, cols]

            @pl.when(jnp.logical_not(in_pair))
            def _():
                kf[...] = k_before[:, cols]
                vf[...] = jnp.zeros_like(vf)

            for t in range(rows // tile):
                lo, hi = t * tile, (t + 1) * tile
                qt = q_ref[lo:hi, cols]
                s_cur = dot(qt, kc[0:hi, cols], ((1,), (1,)))
                s_prev = dot(qt, kp[lo:, cols], ((1,), (1,))) + prev_floor
                s_full = dot(qt, kf[...], ((1,), (1,))) + full_floor
                s_rest = [jnp.where(causal, s_cur[:, lo:hi], s_prev[:, :tile]), s_full]
                if lo:
                    s_rest.append(s_cur[:, :lo])
                if hi < rows:
                    s_rest.append(s_prev[:, tile:])
                top = s_rest[0].max(axis=1, keepdims=True)
                for s in s_rest[1:]:
                    top = jnp.maximum(top, s.max(axis=1, keepdims=True))
                es = [jnp.exp2((s - top) * scale) for s in s_rest]
                total = es[0].sum(axis=1, keepdims=True)
                for e in es[1:]:
                    total += e.sum(axis=1, keepdims=True)
                share = 1.0 / total
                e_cur = jnp.where(causal, es[0], 0.0).astype(BF16)
                acc = dot(e_cur, vc[lo:hi, cols], ((1,), (0,)))
                acc += dot(es[1].astype(BF16), vf[...], ((1,), (0,)))
                if lo:
                    acc += dot(es[2].astype(BF16), vc[:lo, cols], ((1,), (0,)))
                    p_ref[at, lo:hi, :lo] = jnp.zeros((tile, lo), BF16)
                p_ref[at, lo:hi, lo:hi] = jnp.where(causal, 0.0, es[0] * share).astype(BF16)
                if hi < rows:
                    p_ref[at, lo:hi, hi:rows] = (es[-1] * share).astype(BF16)
                p_ref[at, lo:hi, rows:] = (es[1] * share).astype(BF16)
                o_ref[lo:hi, outs] = acc * share
            return carry

        lax.fori_loop(0, number, one_head, 0)

    return call(
        body,
        [SM] + [VM] * 7,
        [sds((rows, number * ADIM), F32), sds((number, rows, 2 * rows), BF16)],
        (info, *arrays),
        scratch=[pltpu.VMEM((rows, ADIM), BF16)] * 2,
    )


def assemble(info, own_parts, oth_parts, cuts):
    rows = own_parts[0].shape[0]
    width = cuts[-1][1]
    count = len(cuts)

    def body(info_ref, *refs):
        parts, out, sem = refs[: 2 * count], refs[2 * count], refs[2 * count + 1]
        copies = []
        for at, ref in enumerate(parts):
            side = info_ref[0] if at < count else 1 - info_ref[0]
            lo, hi = cuts[at % count]
            start = pl.multiple_of(side * width + lo, ADIM)
            copies.append(
                pltpu.make_async_copy(ref, out.at[:, pl.ds(start, hi - lo)], sem.at[at])
            )
        for copy in copies:
            copy.start()
        for copy in copies:
            copy.wait()

    return call(
        body,
        [SM] + [VM] * (2 * count),
        [sds((rows, 2 * width), BF16)],
        (info, *own_parts, *oth_parts),
        out_specs=[HBM],
        scratch=[pltpu.SemaphoreType.DMA((2 * count,))],
    )[0]


def rate_rows(info, step_size):
    rows = step_size.shape[0]

    def body(info_ref, step_ref, own_ref, send_ref):
        both = jnp.transpose(step_ref[...])
        upper = info_ref[0] == 1
        own_ref[...] = jnp.broadcast_to(jnp.where(upper, both[1:2], both[0:1]), (8, rows))
        send_ref[...] = jnp.broadcast_to(jnp.where(upper, both[0:1], both[1:2]), (8, rows))

    return call(body, [SM, VM], [sds((8, rows), F32)] * 2, (info, step_size))


def layer(qkv, step_size, fast_in, fast_out):
    _, tok_rows, _ = qkv.shape
    head_width = fast_in.shape[1]
    hidden_dim = fast_out.shape[1]
    ctx_count = lax.axis_size("ctx")
    line = ctx_count // 2
    index = lax.axis_index("ctx").astype(jnp.int32)
    keep = index % 2
    place = index // 2
    inner = ((place == line // 2) | (place == line // 2 - 1)).astype(jnp.int32)
    info = jnp.stack([keep, place, inner])
    factor = (tok_rows * ctx_count) ** (-0.5)

    swap_pairs = [(i, i ^ 1) for i in range(ctx_count)]
    next_pairs = [(i, i + 2) for i in range(ctx_count - 2)]

    def along(moves):
        return [(2 * a + y, 2 * b + y) for a, b in moves for y in (0, 1)]

    def permute(array, pairs):
        return lax.ppermute(array, "ctx", pairs)

    parts = 4
    part = hidden_dim // parts
    in_cuts = [(i * part, (i + 1) * part) for i in range(parts)]
    middle = (head_width // ADIM + 1) // 2 * ADIM
    out_cuts = [(0, middle), (middle, head_width)]

    qkv = pltpu.with_memory_space_constraint(qkv, pltpu.HBM)
    (k_away,) = cut_blocks(info, qkv, [(1, False)], head_width)
    k_oth = permute(k_away, swap_pairs)
    (k_own,) = cut_blocks(info, qkv, [(1, True)], head_width)
    pk_own = permute(k_own, next_pairs)
    v_away, v_own = cut_blocks(info, qkv, [(2, False), (2, True)], head_width)
    rate_own, rate_send = rate_rows(info, step_size)
    rate_oth = permute(rate_send, swap_pairs)
    v_oth = permute(v_away, swap_pairs)
    q_away, q_own = cut_blocks(info, qkv, [(0, False), (0, True)], head_width)
    q_oth = permute(q_away, swap_pairs)
    pk_oth = permute(k_oth, next_pairs)
    if line == 4:
        own_early = permute(v_own, along([(1, 2), (2, 3)]))
        oth_early = permute(v_oth, along([(2, 3)]))
        stacks, singles = late_columns(v_own, v_oth, out_cuts)
        late_vals = []
        for i, (lo, hi) in enumerate(out_cuts):
            first = permute(stacks[i], along([(0, 1)]))
            second = permute(singles[i], along([(1, 2)]))
            late_vals.append((
                [(own_early, 0, None), (first, lo, 0)],
                [(oth_early, 0, None), (first, lo, 1), (second, lo, None)],
            ))
    else:
        late_vals = [(
            [(permute(v_own, next_pairs), 0, None)], [(permute(v_oth, next_pairs), 0, None)]
        )] * len(out_cuts)

    gin, gout = grads_own(info, k_own, v_own, rate_own, fast_in, fast_out)
    gates = pair_gates(info, k_oth, fast_in, hidden_dim)
    scaled, *first = pair_first(gates[0], v_oth, rate_oth, gout, *out_cuts[0])
    send, kept = pair_grads(
        info, k_oth, scaled, fast_out, gates, gin, gout, in_cuts, out_cuts[1:]
    )
    send, kept = [first[0], *send], [first[1], *kept]
    in_norms, out_norms = column_norms(info, fast_in, fast_out)
    plan = [(fast_out, out_norms, *out_cuts[0], False)]
    plan += [(fast_in, in_norms, lo, hi, True) for lo, hi in in_cuts]
    plan += [(fast_out, out_norms, lo, hi, False) for lo, hi in out_cuts[1:]]

    made, got = [], []
    if line == 4:
        inward = along([(0, 1), (3, 2)])
        centre = along([(1, 2), (2, 1)])
        outward = along([(1, 0), (2, 3)])
        arrived = [permute(array, inward) for array in send]
        for at, (fast, norms, lo, hi, paired) in enumerate(plan):
            first = kept[at - 1].shape[0] if at == len(send) else 0
            source = arrived[min(at, len(send) - 1)]
            half_sum, total = add_chunk(kept[at], source, first)
            crossed = [permute(half_sum, centre)]
            made.append(new_weights(info, total, crossed, fast, norms, lo, hi, factor, paired))
            got.append(permute(made[at], outward))
    else:
        for at, (fast, norms, lo, hi, paired) in enumerate(plan):
            slots = jnp.where(jnp.arange(2)[:, None, None] == keep, kept[at][None], 0.0)
            total = lax.dynamic_index_in_dim(lax.psum(slots, "ctx"), keep, 0, keepdims=False)
            made.append(new_weights(info, total, (), fast, norms, lo, hi, factor, paired))
        got = made

    heads = head_width // ADIM
    split = middle // ADIM
    blocks = (k_own, v_own, k_oth, v_oth, pk_own, pk_oth)
    own_sum, own_p = attention(info, 0, (0, heads), q_own, *blocks)
    oth_some = attention(info, 1, (0, split), q_oth, *blocks)
    oth_rest = attention(info, 1, (split, heads), q_oth, *blocks)
    hiddens = [query_hidden(info, q_own, q_oth, made[i], got[i]) for i in range(1, 1 + parts)]
    own_parts, oth_parts = [], []
    for i, (lo, hi) in enumerate(out_cuts):
        at = parts + i if i else 0
        some = (hiddens, made[at], got[at])
        if lo < middle:
            left = (oth_some[0], lo, oth_some[1])
        else:
            left = (oth_rest[0], lo - middle, oth_rest[1])
        theirs = apply_chunk(info, 1, *some, left, late_vals[i], lo, hi)
        oth_parts.append(permute(theirs, swap_pairs))
        left = (own_sum, lo, own_p)
        own_parts.append(apply_chunk(info, 0, *some, left, late_vals[i], lo, hi))
    return assemble(info, own_parts, oth_parts, out_cuts)


def solution(mesh):
    placed = (
        P(None, "ctx", "head"),
        P("ctx", "head"),
        P("head", None, None),
        P("head", None, None),
    )
    return jax.shard_map(
        layer, mesh=mesh, in_specs=placed, out_specs=P("ctx", "head"), check_vma=False
    )
```

```python
import math

import jax
import jax.numpy as jnp
from jax import lax
from jax.experimental import pallas as pl
from jax.experimental.pallas import tpu as pltpu
from jax.sharding import PartitionSpec as P


ADIM = 128
EPS = 1e-06
F32 = jnp.float32
BF16 = jnp.bfloat16
PIECES = 1
VMEM_LIMIT = 20 * 1024 * 1024


VM = pl.BlockSpec(memory_space=pltpu.VMEM)
SM = pl.BlockSpec(memory_space=pltpu.SMEM)
HBM = pl.BlockSpec(memory_space=pltpu.HBM)


def sds(shape, dtype):
    return jax.ShapeDtypeStruct(shape, dtype)


def call(body, ins, outs, args, out_specs=None, scratch=()):
    return pl.pallas_call(
        body,
        in_specs=ins,
        out_specs=out_specs if out_specs is not None else [VM] * len(outs),
        out_shape=outs,
        scratch_shapes=list(scratch),
        compiler_params=pltpu.CompilerParams(vmem_limit_bytes=VMEM_LIMIT),
    )(*args)


def dot(a, b, dims):
    return lax.dot_general(a, b, (dims, ((), ())), preferred_element_type=F32)


def cut_blocks(info, qkv, picks, width):
    rows = qkv.shape[1]
    count = len(picks)

    def body(info_ref, qkv_ref, *rest):
        outs, sem = rest[:count], rest[count]
        copies = []
        for at, (which, own) in enumerate(picks):
            side = info_ref[0] if own else 1 - info_ref[0]
            cols = pl.ds(pl.multiple_of(side * width, ADIM), width)
            for piece in range(PIECES):
                some = pl.ds(piece * (rows // PIECES), rows // PIECES)
                copies.append(
                    pltpu.make_async_copy(
                        qkv_ref.at[which, some, cols], outs[at].at[some, :], sem.at[at, piece]
                    )
                )
        for copy in copies:
            copy.start()
        for copy in copies:
            copy.wait()

    return call(
        body,
        [SM, HBM],
        [sds((rows, width), BF16)] * count,
        (info, qkv),
        scratch=[pltpu.SemaphoreType.DMA((count, PIECES))],
    )


def late_columns(first, second, cuts):
    count = len(cuts)

    def body(a_ref, b_ref, *outs):
        for (lo, hi), stack, single in zip(cuts, outs, outs[count:]):
            stack[0] = a_ref[:, lo:hi]
            stack[1] = b_ref[:, lo:hi]
            single[...] = b_ref[:, lo:hi]

    rows = first.shape[0]
    shapes = [(2, rows, hi - lo) for lo, hi in cuts] + [(rows, hi - lo) for lo, hi in cuts]
    outs = call(body, [VM] * 2, [sds(shape, BF16) for shape in shapes], (first, second))
    return outs[:count], outs[count:]


def gate_parts(keys, w_in, hidden_dim):
    projected = dot(keys, w_in, ((1,), (0,)))
    gate = projected[:, :hidden_dim]
    up = projected[:, hidden_dim:]
    sig = jax.nn.sigmoid(gate)
    act = gate * sig
    slope = sig * (1.0 + gate * (1.0 - sig))
    return (act * up).astype(BF16), up * slope, act


def scale_rows(vals, rate_rows):
    return (jnp.transpose(rate_rows)[:, :1] * vals.astype(F32)).astype(BF16)


def back_parts(scaled, w_out, tilt, act):
    back = dot(scaled, w_out, ((1,), (1,)))
    return (back * tilt).astype(BF16), (back * act).astype(BF16)


def grads_own(info, keys, vals, rates, fast_in, fast_out):
    width = keys.shape[1]
    hidden_dim = fast_out.shape[1]

    def body(info_ref, k_ref, v_ref, rate_ref, win_ref, wout_ref, gin_ref, gout_ref):
        keep = info_ref[0]
        hidden, tilt, act = gate_parts(k_ref[...], win_ref[keep], hidden_dim)
        scaled = scale_rows(v_ref[...], rate_ref[...])
        pre_gate, pre_up = back_parts(scaled, wout_ref[keep], tilt, act)
        gin_ref[:, :hidden_dim] = dot(k_ref[...], pre_gate, ((0,), (0,)))
        gin_ref[:, hidden_dim:] = dot(k_ref[...], pre_up, ((0,), (0,)))
        gout_ref[...] = dot(hidden, scaled, ((0,), (0,)))

    return call(
        body,
        [SM] + [VM] * 5,
        [sds((width, 2 * hidden_dim), F32), sds((hidden_dim, width), F32)],
        (info, keys, vals, rates, fast_in, fast_out),
    )


def pair_gates(info, keys, fast_in, hidden_dim):
    rows = keys.shape[0]

    def body(info_ref, k_ref, win_ref, hid_ref, tilt_ref, act_ref):
        hidden, tilt, act = gate_parts(k_ref[...], win_ref[info_ref[0]], hidden_dim)
        hid_ref[...] = hidden
        tilt_ref[...] = tilt
        act_ref[...] = act

    shape = (rows, hidden_dim)
    return call(
        body,
        [SM, VM, VM],
        [sds(shape, BF16), sds(shape, F32), sds(shape, F32)],
        (info, keys, fast_in),
    )


def pair_first(hidden, vals, rates, gout, lo, hi):
    def body(h_ref, v_ref, rate_ref, gout_ref, scaled_ref, send_ref, kept_ref):
        scaled = scale_rows(v_ref[...], rate_ref[...])
        scaled_ref[...] = scaled
        part = gout_ref[:, lo:hi] + dot(h_ref[...], scaled[:, lo:hi], ((0,), (0,)))
        send_ref[...] = part.astype(BF16)
        kept_ref[...] = part

    shape = (gout.shape[0], hi - lo)
    return call(
        body,
        [VM] * 4,
        [sds(vals.shape, BF16), sds(shape, BF16), sds(shape, F32)],
        (hidden, vals, rates, gout),
    )


def pair_grads(info, keys, scaled, fast_out, gates, gin, gout, in_cuts, out_cuts):
    width = keys.shape[1]
    hidden_dim = fast_out.shape[1]
    count = len(in_cuts) + len(out_cuts)

    def body(info_ref, k_ref, s_ref, wout_ref, h_ref, t_ref, a_ref, gin_ref, gout_ref, *o):
        sends = [o[i] for i in range(count - 2)]
        sends += [o[count - 2].at[:width, :], o[count - 2].at[width:, :]]
        keeps = o[count - 1 :]
        pre_gate, pre_up = back_parts(s_ref[...], wout_ref[info_ref[0]], t_ref[...], a_ref[...])
        for at, (lo, hi) in enumerate(in_cuts):
            size = hi - lo
            for start, base, pre in ((0, lo, pre_gate), (size, hidden_dim + lo, pre_up)):
                part = gin_ref[:, base : base + size]
                part += dot(k_ref[...], pre[:, lo:hi], ((0,), (0,)))
                sends[at][:, start : start + size] = part.astype(BF16)
                keeps[at][:, start : start + size] = part
        for at, (lo, hi) in enumerate(out_cuts, len(in_cuts)):
            part = gout_ref[:, lo:hi] + dot(h_ref[...], s_ref[:, lo:hi], ((0,), (0,)))
            sends[at][...] = part.astype(BF16)
            keeps[at][...] = part

    shapes = [(width, 2 * (hi - lo)) for lo, hi in in_cuts]
    shapes += [(hidden_dim, hi - lo) for lo, hi in out_cuts]
    joined = (shapes[-2][0] + shapes[-1][0], shapes[-1][1])
    outs = call(
        body,
        [SM] + [VM] * 8,
        [sds(s, BF16) for s in shapes[:-2] + [joined]] + [sds(s, F32) for s in shapes],
        (info, keys, scaled, fast_out, *gates, gin, gout),
    )
    return outs[: count - 1], outs[count - 1 :]


def add_chunk(kept, got, first):
    rows = kept.shape[0]

    def body(kept_ref, got_ref, send_ref, sum_ref):
        total = kept_ref[...] + got_ref[first : first + rows, :].astype(F32)
        send_ref[...] = total.astype(BF16)
        sum_ref[...] = total

    return call(body, [VM] * 2, [sds(kept.shape, BF16), sds(kept.shape, F32)], (kept, got))


def column_norms(info, fast_in, fast_out):
    def body(info_ref, win_ref, wout_ref, in_ref, out_ref):
        for ref, out in ((win_ref, in_ref), (wout_ref, out_ref)):
            old = ref[info_ref[0]].astype(F32)
            out[...] = jnp.sqrt(jnp.sum(old * old, axis=0, keepdims=True))

    return call(
        body,
        [SM, VM, VM],
        [sds((1, fast_in.shape[2]), F32), sds((1, fast_out.shape[2]), F32)],
        (info, fast_in, fast_out),
    )


def new_weights(info, mine, others, fast, norms, lo, hi, factor, paired):
    count = len(others)
    size = hi - lo
    half = fast.shape[2] // 2

    def body(info_ref, a_ref, *rest):
        w_ref, norm_ref, o_ref = rest[count:]
        keep = info_ref[0]
        spans = [(0, lo)] + ([(size, half + lo)] if paired else [])
        for start, col in spans:
            total = a_ref[:, start : start + size]
            for b_ref in rest[:count]:
                total += b_ref[:, start : start + size].astype(F32)
            moved = w_ref[keep, :, col : col + size].astype(F32) + total * factor
            new_norm = jnp.sqrt(jnp.sum(moved * moved, axis=0, keepdims=True))
            ratio = norm_ref[:, col : col + size] / (new_norm + EPS)
            o_ref[:, start : start + size] = (moved * ratio).astype(BF16)

    return call(
        body, [SM] + [VM] * (count + 3), [sds(mine.shape, BF16)], (info, mine, *others, fast, norms)
    )[0]


def query_hidden(info, q_own, q_oth, made, got):
    rows = q_own.shape[0]
    size = made.shape[1] // 2

    def body(info_ref, qa_ref, qb_ref, made_ref, got_ref, o_ref):
        def run(w_ref):
            for start, ref in ((0, qa_ref), (rows, qb_ref)):
                proj = dot(ref[...], w_ref[...], ((1,), (0,)))
                gate = proj[:, :size]
                o_ref[start : start + rows, :] = (
                    gate * jax.nn.sigmoid(gate) * proj[:, size:]
                ).astype(BF16)

        @pl.when(info_ref[2] == 1)
        def _():
            run(made_ref)

        @pl.when(info_ref[2] != 1)
        def _():
            run(got_ref)

    return call(
        body, [SM] + [VM] * 4, [sds((2 * rows, size), BF16)], (info, q_own, q_oth, made, got)
    )[0]


def apply_chunk(info, side, hiddens, made, got, left, late, lo, hi):
    rows = hiddens[0].shape[0] // 2
    size = hi - lo
    count = len(hiddens)
    sums, base, weights = left
    vals = [array for group in late for array, _, _ in group]

    def body(info_ref, *refs):
        hid = refs[:count]
        made_ref, got_ref = refs[count : count + 2]
        val_refs = list(refs[count + 2 : count + 2 + len(vals)])
        sum_ref, p_ref, out = refs[-3:]
        groups = [[(val_refs.pop(0), *place) for _, *place in group] for group in late]

        def values(group, head):
            total = None
            for ref, first, layer_at in group:
                col = lo - first + head * ADIM
                cols = slice(col, col + ADIM)
                piece = ref[:, cols] if layer_at is None else ref[layer_at, :, cols]
                total = piece if total is None else total + piece
            return total

        def run(w_ref):
            total = sum_ref[:, base : base + size]
            row = 0
            for ref in hid:
                part = ref.shape[1]
                total += dot(
                    ref[side * rows : (side + 1) * rows, :], w_ref[row : row + part, :], ((1,), (0,))
                )
                row += part
            for head in range(size // ADIM):
                col = head * ADIM
                mixed = total[:, col : col + ADIM]
                for place, which in enumerate((side, 1 - side)):
                    p = p_ref[base // ADIM + head, :, place * rows : (place + 1) * rows]
                    v = values(groups[which], head)
                    if place == 1:
                        v = jnp.where(info_ref[0] == which, jnp.zeros_like(v), v)
                    mixed += dot(p, v, ((1,), (0,)))
                out[:, col : col + ADIM] = mixed.astype(BF16)

        @pl.when(info_ref[2] == 1)
        def _():
            run(made_ref)

        @pl.when(info_ref[2] != 1)
        def _():
            run(got_ref)

    return call(
        body,
        [SM] + [VM] * (count + 2 + len(vals) + 2),
        [sds((rows, size), BF16)],
        (info, *hiddens, made, got, *vals, sums, weights),
    )[0]


def attention(info, side, heads, q, k_own, v_own, k_oth, v_oth, pk_own, pk_oth):
    rows = q.shape[0]
    tile = min(256, rows)
    first, last = heads
    number = last - first
    scale = ADIM ** (-0.5) * math.log2(math.e)
    if side == 0:
        arrays = (q, k_own, v_own, pk_own, k_oth, v_oth, pk_oth)
    else:
        arrays = (q, k_oth, v_oth, pk_oth, k_own, v_own, pk_own)

    def body(info_ref, q_ref, kc, vc, kp, k_pair, v_pair, k_before, o_ref, p_ref, kf, vf):
        has_prev = info_ref[1] > 0
        in_pair = info_ref[0] == 1 - side
        row = lax.broadcasted_iota(jnp.int32, (tile, tile), 0)
        col = lax.broadcasted_iota(jnp.int32, (tile, tile), 1)
        causal = col <= row
        prev_floor = jnp.where(has_prev, 0.0, -1e30)
        full_floor = jnp.where(jnp.logical_or(in_pair, has_prev), 0.0, -1e30)

        def one_head(at, carry):
            cols = pl.ds(pl.multiple_of((first + at) * ADIM, ADIM), ADIM)
            outs = pl.ds(pl.multiple_of(at * ADIM, ADIM), ADIM)

            @pl.when(in_pair)
            def _():
                kf[...] = k_pair[:, cols]
                vf[...] = v_pair[:, cols]

            @pl.when(jnp.logical_not(in_pair))
            def _():
                kf[...] = k_before[:, cols]
                vf[...] = jnp.zeros_like(vf)

            for t in range(rows // tile):
                lo, hi = t * tile, (t + 1) * tile
                qt = q_ref[lo:hi, cols]
                s_cur = dot(qt, kc[0:hi, cols], ((1,), (1,)))
                s_prev = dot(qt, kp[lo:, cols], ((1,), (1,))) + prev_floor
                s_full = dot(qt, kf[...], ((1,), (1,))) + full_floor
                s_rest = [jnp.where(causal, s_cur[:, lo:hi], s_prev[:, :tile]), s_full]
                if lo:
                    s_rest.append(s_cur[:, :lo])
                if hi < rows:
                    s_rest.append(s_prev[:, tile:])
                top = s_rest[0].max(axis=1, keepdims=True)
                for s in s_rest[1:]:
                    top = jnp.maximum(top, s.max(axis=1, keepdims=True))
                es = [jnp.exp2((s - top) * scale) for s in s_rest]
                total = es[0].sum(axis=1, keepdims=True)
                for e in es[1:]:
                    total += e.sum(axis=1, keepdims=True)
                share = 1.0 / total
                e_cur = jnp.where(causal, es[0], 0.0).astype(BF16)
                acc = dot(e_cur, vc[lo:hi, cols], ((1,), (0,)))
                acc += dot(es[1].astype(BF16), vf[...], ((1,), (0,)))
                if lo:
                    acc += dot(es[2].astype(BF16), vc[:lo, cols], ((1,), (0,)))
                    p_ref[at, lo:hi, :lo] = jnp.zeros((tile, lo), BF16)
                p_ref[at, lo:hi, lo:hi] = jnp.where(causal, 0.0, es[0] * share).astype(BF16)
                if hi < rows:
                    p_ref[at, lo:hi, hi:rows] = (es[-1] * share).astype(BF16)
                p_ref[at, lo:hi, rows:] = (es[1] * share).astype(BF16)
                o_ref[lo:hi, outs] = acc * share
            return carry

        lax.fori_loop(0, number, one_head, 0)

    return call(
        body,
        [SM] + [VM] * 7,
        [sds((rows, number * ADIM), F32), sds((number, rows, 2 * rows), BF16)],
        (info, *arrays),
        scratch=[pltpu.VMEM((rows, ADIM), BF16)] * 2,
    )


def assemble(info, own_parts, oth_parts, cuts):
    rows = own_parts[0].shape[0]
    width = cuts[-1][1]
    count = len(cuts)

    def body(info_ref, *refs):
        parts, out, sem = refs[: 2 * count], refs[2 * count], refs[2 * count + 1]
        copies = []
        for at, ref in enumerate(parts):
            side = info_ref[0] if at < count else 1 - info_ref[0]
            lo, hi = cuts[at % count]
            start = pl.multiple_of(side * width + lo, ADIM)
            copies.append(
                pltpu.make_async_copy(ref, out.at[:, pl.ds(start, hi - lo)], sem.at[at])
            )
        for copy in copies:
            copy.start()
        for copy in copies:
            copy.wait()

    return call(
        body,
        [SM] + [VM] * (2 * count),
        [sds((rows, 2 * width), BF16)],
        (info, *own_parts, *oth_parts),
        out_specs=[HBM],
        scratch=[pltpu.SemaphoreType.DMA((2 * count,))],
    )[0]


def rate_rows(info, step_size):
    rows = step_size.shape[0]

    def body(info_ref, step_ref, own_ref, send_ref):
        both = jnp.transpose(step_ref[...])
        upper = info_ref[0] == 1
        own_ref[...] = jnp.broadcast_to(jnp.where(upper, both[1:2], both[0:1]), (8, rows))
        send_ref[...] = jnp.broadcast_to(jnp.where(upper, both[0:1], both[1:2]), (8, rows))

    return call(body, [SM, VM], [sds((8, rows), F32)] * 2, (info, step_size))


def layer(qkv, step_size, fast_in, fast_out):
    _, tok_rows, _ = qkv.shape
    head_width = fast_in.shape[1]
    hidden_dim = fast_out.shape[1]
    ctx_count = lax.axis_size("ctx")
    line = ctx_count // 2
    index = lax.axis_index("ctx").astype(jnp.int32)
    keep = index % 2
    place = index // 2
    inner = ((place == line // 2) | (place == line // 2 - 1)).astype(jnp.int32)
    info = jnp.stack([keep, place, inner])
    factor = (tok_rows * ctx_count) ** (-0.5)

    swap_pairs = [(i, i ^ 1) for i in range(ctx_count)]
    next_pairs = [(i, i + 2) for i in range(ctx_count - 2)]

    def along(moves):
        return [(2 * a + y, 2 * b + y) for a, b in moves for y in (0, 1)]

    def permute(array, pairs):
        return lax.ppermute(array, "ctx", pairs)

    parts = 4
    part = hidden_dim // parts
    in_cuts = [(i * part, (i + 1) * part) for i in range(parts)]
    middle = (head_width // ADIM + 1) // 2 * ADIM
    out_cuts = [(0, middle), (middle, head_width)]

    qkv = pltpu.with_memory_space_constraint(qkv, pltpu.HBM)
    (k_away,) = cut_blocks(info, qkv, [(1, False)], head_width)
    k_oth = permute(k_away, swap_pairs)
    (k_own,) = cut_blocks(info, qkv, [(1, True)], head_width)
    pk_own = permute(k_own, next_pairs)
    v_away, v_own = cut_blocks(info, qkv, [(2, False), (2, True)], head_width)
    rate_own, rate_send = rate_rows(info, step_size)
    rate_oth = permute(rate_send, swap_pairs)
    v_oth = permute(v_away, swap_pairs)
    q_away, q_own = cut_blocks(info, qkv, [(0, False), (0, True)], head_width)
    q_oth = permute(q_away, swap_pairs)
    pk_oth = permute(k_oth, next_pairs)
    if line == 4:
        own_early = permute(v_own, along([(1, 2), (2, 3)]))
        oth_early = permute(v_oth, along([(2, 3)]))
        stacks, singles = late_columns(v_own, v_oth, out_cuts)
        late_vals = []
        for i, (lo, hi) in enumerate(out_cuts):
            first = permute(stacks[i], along([(0, 1)]))
            second = permute(singles[i], along([(1, 2)]))
            late_vals.append((
                [(own_early, 0, None), (first, lo, 0)],
                [(oth_early, 0, None), (first, lo, 1), (second, lo, None)],
            ))
    else:
        late_vals = [(
            [(permute(v_own, next_pairs), 0, None)], [(permute(v_oth, next_pairs), 0, None)]
        )] * len(out_cuts)

    gin, gout = grads_own(info, k_own, v_own, rate_own, fast_in, fast_out)
    gates = pair_gates(info, k_oth, fast_in, hidden_dim)
    scaled, *first = pair_first(gates[0], v_oth, rate_oth, gout, *out_cuts[0])
    send, kept = pair_grads(
        info, k_oth, scaled, fast_out, gates, gin, gout, in_cuts, out_cuts[1:]
    )
    send, kept = [first[0], *send], [first[1], *kept]
    in_norms, out_norms = column_norms(info, fast_in, fast_out)
    plan = [(fast_out, out_norms, *out_cuts[0], False)]
    plan += [(fast_in, in_norms, lo, hi, True) for lo, hi in in_cuts]
    plan += [(fast_out, out_norms, lo, hi, False) for lo, hi in out_cuts[1:]]

    made, got = [], []
    if line == 4:
        inward = along([(0, 1), (3, 2)])
        centre = along([(1, 2), (2, 1)])
        outward = along([(1, 0), (2, 3)])
        arrived = [permute(array, inward) for array in send]
        for at, (fast, norms, lo, hi, paired) in enumerate(plan):
            first = kept[at - 1].shape[0] if at == len(send) else 0
            source = arrived[min(at, len(send) - 1)]
            half_sum, total = add_chunk(kept[at], source, first)
            crossed = [permute(half_sum, centre)]
            made.append(new_weights(info, total, crossed, fast, norms, lo, hi, factor, paired))
            got.append(permute(made[at], outward))
    else:
        for at, (fast, norms, lo, hi, paired) in enumerate(plan):
            slots = jnp.where(jnp.arange(2)[:, None, None] == keep, kept[at][None], 0.0)
            total = lax.dynamic_index_in_dim(lax.psum(slots, "ctx"), keep, 0, keepdims=False)
            made.append(new_weights(info, total, (), fast, norms, lo, hi, factor, paired))
        got = made

    heads = head_width // ADIM
    split = middle // ADIM
    blocks = (k_own, v_own, k_oth, v_oth, pk_own, pk_oth)
    own_some = attention(info, 0, (0, split), q_own, *blocks)
    own_rest = attention(info, 0, (split, heads), q_own, *blocks)
    oth_some = attention(info, 1, (0, split), q_oth, *blocks)
    oth_rest = attention(info, 1, (split, heads), q_oth, *blocks)
    hiddens = [query_hidden(info, q_own, q_oth, made[i], got[i]) for i in range(1, 1 + parts)]
    own_parts, oth_parts = [], []
    for i, (lo, hi) in enumerate(out_cuts):
        at = parts + i if i else 0
        some = (hiddens, made[at], got[at])
        first, place = lo < middle, lo if lo < middle else lo - middle
        own_left = own_some if first else own_rest
        oth_left = oth_some if first else oth_rest
        left = (oth_left[0], place, oth_left[1])
        theirs = apply_chunk(info, 1, *some, left, late_vals[i], lo, hi)
        oth_parts.append(permute(theirs, swap_pairs))
        left = (own_left[0], place, own_left[1])
        own_parts.append(apply_chunk(info, 0, *some, left, late_vals[i], lo, hi))
    return assemble(info, own_parts, oth_parts, out_cuts)


def solution(mesh):
    placed = (
        P(None, "ctx", "head"),
        P("ctx", "head"),
        P("head", None, None),
        P("head", None, None),
    )
    return jax.shard_map(
        layer, mesh=mesh, in_specs=placed, out_specs=P("ctx", "head"), check_vma=False
    )
```
